256 devices in a mesh: dp: 8 (over z), tenant: 32 (over y, x, core).
Axes of the slice: x: 4, y: 4, z: 8, core: 2. Of those that a mesh axis runs over, the one named last changes fastest.
Arguments:
- tokens: bfloat16 [2048, 8192], P(('dp', 'tenant')), may hold values from -6 to 6
- tenant_ids: int32 [8, 256], P('dp', 'tenant'), may hold values from 0 to 31, never falling along the last dimension, each value on 1 to 16 neighbouring positions
- gate_weight: bfloat16 [8192, 16384], P('dp', 'tenant'), may hold values from -0.0625 to 0.0625
- up_weight: bfloat16 [8192, 16384], P('dp', 'tenant'), may hold values from -0.0625 to 0.0625
- adapter_in: bfloat16 [32, 32, 8192], P('tenant'), may hold values from -0.0625 to 0.0625
- adapter_out: bfloat16 [32, 2, 16, 16384], P('tenant'), may hold values from -0.75 to 0.75
- grad_hidden: bfloat16 [2048, 16384], P('dp', 'tenant'), may hold values from -6 to 6
Outputs:
- hidden: bfloat16 [2048, 16384], P('dp', 'tenant')
- grad_tokens: bfloat16 [2048, 8192], P(('dp', 'tenant'))
- grad_in: float32 [32, 32, 8192], P('tenant', None, 'dp')
- grad_out: float32 [32, 2, 16, 16384], P('tenant', None, None, 'dp')
The draws below stay inside these ranges and needn't reach their ends.
Inputs may be any that keep to these rules, and one draw needn't show every extreme that they name: `tenant_ids`: within each batch the tenant numbers never fall along the row; every tenant has 1 to 16 tokens in each batch, and some tenant exactly 16.
All inputs are finite; a program needn't handle non-finite values.
Results may differ from the reference program's by a relative error of at most 0.019.
Values may be sent and summed in bfloat16 or wider, within the bound.
No kernel may reach another device: no remote copies, remote signals or barrier semaphores. Data moves between devices by JAX's collectives and lax.ppermute only.
A program may use at most 128 MiB of HBM per device.

```python
import math
import jax
import jax.numpy as jnp
import numpy as np
from jax import lax

D = 8192
FF = 16384
R = 16
GROUPS = 8
GROUP = 256
TOKENS = 2048
TENANTS = 32
CAPT = 16
N_TENANT = 32


def levels(key, dims, pieces, low, largest):
    def one(position, blocks):
        steps = jax.random.uniform(jax.random.fold_in(jax.random.fold_in(key, 6), position), (blocks,), jnp.float32, low / len(pieces), largest / len(pieces))
        return jnp.repeat(jnp.exp(steps), dims[position] // blocks).reshape((-1,) + (1,) * (len(dims) - position - 1))

    loudness = one(*pieces[0])
    for cut in pieces[1:]:
        loudness = loudness * one(*cut)
    return loudness


def profile(number_of, total, limit, slope):
    weights = [(1 << 20) // math.isqrt(grade ** slope) + 1 for grade in range(2, number_of + 1)]
    surplus, holding = total - limit - (number_of - 1), [1] * (number_of - 1)
    while surplus > 0:
        candidates = [i for i in range(number_of - 1) if holding[i] < limit]
        whole, left = sum([weights[i] for i in candidates]), surplus
        for i in candidates:
            addition = min(limit - holding[i], max(1, left * weights[i] // whole), surplus)
            holding[i] = holding[i] + addition
            surplus = surplus - addition
    return np.array([limit] + holding)


def uneven_parts(stream_key, number_of, total, most, slope):
    if number_of == 2:
        one = jax.random.randint(stream_key, (), max(1, total - most), min(most, total - 1) + 1)
        return jnp.stack([one, total - one])
    tallies = jnp.asarray(profile(number_of, total, most, slope), jnp.int32)
    twos = (number_of - 1) // 2
    giver, receiver = tallies[1:1 + 2 * twos:2], tallies[2:2 + 2 * twos:2]
    slack = jnp.minimum(giver - 1, most - receiver)
    shifted = jax.random.randint(jax.random.fold_in(stream_key, 1), (twos,), 0, 1 << 20) % (slack + 1)
    tallies = tallies.at[1:1 + 2 * twos:2].set(giver - shifted).at[2:2 + 2 * twos:2].set(receiver + shifted)
    return tallies[jax.random.permutation(jax.random.fold_in(stream_key, 2), number_of)]


def centred(stream_key, shape, spread, reach, cuts=(), kind=jnp.bfloat16):
    level = levels(stream_key, shape, cuts, -0.22, 0.18) if cuts else 1.0
    array = jax.random.normal(stream_key, shape, jnp.float32) * spread * level
    return jnp.minimum(jnp.maximum(array, -reach), reach).astype(kind)


def setup_inputs(seed: int = 0) -> dict:
    arg_keys = jax.random.split(jax.random.key(seed), 8)
    return {
        "tokens": centred(arg_keys[0], (TOKENS, D), 1.0, 6.0, ((0, 256),)),
        "tenant_ids": jax.vmap(lambda own: jnp.searchsorted(jnp.cumsum(uneven_parts(own, TENANTS, GROUP, CAPT, 2)), jnp.arange(GROUP), side="right"))(jax.random.split(arg_keys[1], GROUPS)).reshape((GROUPS, GROUP)).astype(jnp.int32),
        "gate_weight": centred(arg_keys[2], (D, FF), D ** -0.5, 0.0625, ((0, 8), (1, 32))),
        "up_weight": centred(arg_keys[3], (D, FF), D ** -0.5, 0.0625, ((0, 8), (1, 32))),
        "adapter_in": centred(arg_keys[4], (TENANTS, 2 * R, D), D ** -0.5, 0.0625, ((0, 32),)),
        "adapter_out": centred(arg_keys[5], (TENANTS, 2, R, FF), (4 * R) ** -0.5, 0.75, ((0, 32),)),
        "grad_hidden": centred(arg_keys[6], (TOKENS, FF), 1.0, 6.0, ((0, 8), (1, 32))),
    }


adapter_scale = 2.0


def expand(values, tenant_indicator):
    total_rows = values.shape[0]
    return (tenant_indicator[:, :, None].astype(values.dtype) * values[:, None, :]).reshape(total_rows, -1)


def reference(tokens, tenant_ids, gate_weight, up_weight, adapter_in, adapter_out, grad_hidden):
    owner_tenants = tenant_ids.reshape(-1)
    number_of_tenants = adapter_in.shape[0]
    adapter_inner_rank = adapter_out.shape[2]
    total_rows = tokens.shape[0]
    tenant_indicator = (owner_tenants[:, None] == jnp.arange(number_of_tenants, dtype=jnp.int32)[None, :]).astype(jnp.float32)
    flattened_input = adapter_in.reshape(number_of_tenants * 2 * adapter_inner_rank, -1)
    projected = lax.dot_general(tokens, flattened_input, (((1,), (1,)), ((), ())), preferred_element_type=jnp.float32)
    low_rank = jnp.sum(projected.reshape(total_rows, number_of_tenants, 2 * adapter_inner_rank) * tenant_indicator[:, :, None], axis=1).astype(jnp.bfloat16)
    update_deltas = []
    for member in range(2):
        broadcast_rank_rows = expand(low_rank[:, member * adapter_inner_rank:(member + 1) * adapter_inner_rank], tenant_indicator)
        flattened_output = adapter_out[:, member].reshape(number_of_tenants * adapter_inner_rank, -1)
        update_deltas.append((adapter_scale * jnp.dot(broadcast_rank_rows, flattened_output, preferred_element_type=jnp.float32)).astype(jnp.bfloat16))
    gate_pre = jnp.dot(tokens, gate_weight, preferred_element_type=jnp.float32) + update_deltas[0].astype(jnp.float32)
    up_pre = jnp.dot(tokens, up_weight, preferred_element_type=jnp.float32) + update_deltas[1].astype(jnp.float32)
    sigmoid_gate = jax.nn.sigmoid(gate_pre)
    silu_gate = gate_pre * sigmoid_gate
    hidden = (silu_gate * up_pre).astype(jnp.bfloat16)
    upstream = grad_hidden.astype(jnp.float32)
    grad_gate = (upstream * up_pre * sigmoid_gate * (1.0 + gate_pre * (1.0 - sigmoid_gate))).astype(jnp.bfloat16)
    grad_up = (upstream * silu_gate).astype(jnp.bfloat16)
    rank_gradients = []
    for member, grad_pre in enumerate((grad_gate, grad_up)):
        flattened_output = adapter_out[:, member].reshape(number_of_tenants * adapter_inner_rank, -1)
        mapped_result = lax.dot_general(grad_pre, flattened_output, (((1,), (1,)), ((), ())), preferred_element_type=jnp.float32)
        rank_gradients.append(adapter_scale * jnp.sum(mapped_result.reshape(total_rows, number_of_tenants, adapter_inner_rank) * tenant_indicator[:, :, None], axis=1))
    grad_low = jnp.concatenate(rank_gradients, axis=1).astype(jnp.bfloat16)
    broadcast_gradient = expand(grad_low, tenant_indicator)
    grad_in = lax.dot_general(broadcast_gradient, tokens, (((0,), (0,)), ((), ())), preferred_element_type=jnp.float32).reshape(number_of_tenants, 2 * adapter_inner_rank, -1)
    output_pieces = []
    for member, grad_pre in enumerate((grad_gate, grad_up)):
        broadcast_rank_rows = expand(low_rank[:, member * adapter_inner_rank:(member + 1) * adapter_inner_rank], tenant_indicator)
        matrix_product = lax.dot_general(broadcast_rank_rows, grad_pre, (((0,), (0,)), ((), ())), preferred_element_type=jnp.float32)
        output_pieces.append(adapter_scale * matrix_product.reshape(number_of_tenants, adapter_inner_rank, -1))
    grad_out = jnp.stack(output_pieces, axis=1)
    adapter_input_rows = jnp.dot(broadcast_gradient, flattened_input, preferred_element_type=jnp.float32)
    block_width = gate_weight.shape[1] // N_TENANT

    def add_block(carry, current_block_index):
        column_start = current_block_index * block_width
        gate_cols = lax.dynamic_slice_in_dim(gate_weight, column_start, block_width, 1)
        up_cols = lax.dynamic_slice_in_dim(up_weight, column_start, block_width, 1)
        grad_gate_cols = lax.dynamic_slice_in_dim(grad_gate, column_start, block_width, 1)
        grad_up_cols = lax.dynamic_slice_in_dim(grad_up, column_start, block_width, 1)
        summand_term = lax.dot_general(grad_gate_cols, gate_cols, (((1,), (1,)), ((), ())), preferred_element_type=jnp.float32)
        summand_term = summand_term + lax.dot_general(grad_up_cols, up_cols, (((1,), (1,)), ((), ())), preferred_element_type=jnp.float32)
        summand_term = summand_term + jnp.where((owner_tenants == current_block_index)[:, None], adapter_input_rows, jnp.zeros_like(adapter_input_rows))
        rounded = lax.optimization_barrier(summand_term.astype(jnp.bfloat16))
        return carry + rounded.astype(jnp.float32), None

    summed, _ = lax.scan(add_block, jnp.zeros((total_rows, tokens.shape[1]), jnp.float32), jnp.arange(N_TENANT, dtype=jnp.int32))
    grad_tokens = summed.astype(jnp.bfloat16)
    return (hidden, grad_tokens, grad_in, grad_out)
```

```python
import jax
import jax.numpy as jnp
from jax import lax
from jax.sharding import Mesh, PartitionSpec as P

adapter_scale = 2.0
bf16 = jnp.bfloat16
f32 = jnp.float32
CHIPS = ("y", "x")
CORE = "c"
GROUP = "z"
ORDER = (4, 3, 5, 2, 6, 1, 7, 0)


def contract(a, b, a_dim, b_dim):
    return lax.dot_general(a, b, (((a_dim,), (b_dim,)), ((), ())), preferred_element_type=f32)


def spread(block, axes, count):
    copies = jnp.broadcast_to(block[None], (count,) + block.shape)
    return lax.all_to_all(copies, axes, split_axis=0, concat_axis=0, tiled=True)


def on_device(tokens, tenant_ids, gate_weight, up_weight, adapter_in, adapter_out, grad_hidden):
    groups = lax.axis_size(GROUP)
    chips = lax.axis_size("y") * lax.axis_size("x")
    own_rows, width = tokens.shape
    depth, columns = gate_weight.shape
    rank = adapter_out.shape[2]
    rows = chips * own_rows
    chip_columns = 2 * columns
    z = lax.axis_index(GROUP)
    c = lax.axis_index(CORE)
    u = lax.axis_index("y") * lax.axis_size("x") + lax.axis_index("x")
    first_core = c == 0
    order = jnp.array(ORDER, jnp.int32)
    place_of = [ORDER.index(d) for d in range(groups)]
    group_at = (z + order) % groups
    place_at = jnp.array(place_of, jnp.int32)[(jnp.arange(groups) - z) % groups]
    swap = [(0, 1), (1, 0)]
    up_ring = [(i, (i + 1) % groups) for i in range(groups)]
    down_ring = [(i, (i - 1) % groups) for i in range(groups)]

    def other_core(value):
        return lax.ppermute(value, CORE, swap)

    def both(own, other):
        return jnp.where(first_core, own, other), jnp.where(first_core, other, own)

    ids = jnp.broadcast_to(tenant_ids.reshape(own_rows, 1, 1).astype(bf16), (own_rows, groups, 128))
    wide = jnp.concatenate([tokens.reshape(own_rows, groups, depth), ids], axis=2)
    sliced = lax.all_to_all(
        wide.reshape(own_rows, groups * (depth + 128)), GROUP, split_axis=1, concat_axis=0, tiled=True
    )
    sliced = jnp.take(sliced.reshape(groups, own_rows, depth + 128), group_at, axis=0)
    sliced = sliced.reshape(groups * own_rows, depth + 128)
    count = groups * own_rows
    id_columns = sliced[:, depth:]
    lane = lax.broadcasted_iota(jnp.int32, (count, 128), 1)
    row = lax.broadcasted_iota(jnp.int32, (count, 128), 0)
    id_lanes = jnp.sum(jnp.where(lane == row, id_columns.astype(f32), 0.0), axis=0, keepdims=True)
    id_block = jnp.broadcast_to(jnp.pad(id_lanes.astype(bf16), ((0, 0), (0, depth - 128))), (8, depth))
    gathered = spread(jnp.concatenate([sliced[:, :depth], id_block], axis=0), CHIPS, chips)
    token_rows = gathered[:, :count].reshape(chips, groups, own_rows, depth)
    token_rows = token_rows.transpose(1, 0, 2, 3).reshape(groups * rows, depth)
    row_ids = gathered[:, count, :count].astype(f32).astype(jnp.int32)
    row_ids = row_ids.reshape(chips, groups, own_rows).transpose(1, 0, 2).reshape(groups, rows)

    gates = both(gate_weight, other_core(gate_weight))
    ups = both(up_weight, other_core(up_weight))
    weight = jnp.concatenate(gates + ups, axis=1)
    by_core = grad_hidden.reshape(chips, 2, own_rows, columns)
    keep = lax.dynamic_index_in_dim(by_core, c, 1, keepdims=False)
    give = lax.dynamic_index_in_dim(by_core, 1 - c, 1, keepdims=False)
    upstream = jnp.concatenate(both(keep, other_core(give)), axis=2).reshape(rows, chip_columns)

    inner = lax.dynamic_slice_in_dim(adapter_in[0], z * depth, depth, axis=1)
    inner = jnp.concatenate([inner, other_core(inner)], axis=0)
    outer = lax.all_to_all(
        adapter_out.reshape(2 * rank, -1), CHIPS, split_axis=1, concat_axis=0, tiled=True
    )
    outers = (outer, other_core(outer))
    chip_range = jnp.arange(chips, dtype=jnp.int32)
    outer_tenants = (2 * chip_range + c, 2 * chip_range + 1 - c)
    my_tenants = (2 * u + c, 2 * u + 1 - c)

    def product(first, last):
        return contract(token_rows[first * rows : last * rows], weight, 1, 0)

    start = product(0, 1).astype(bf16)
    going_up = lax.ppermute(start[:, :chip_columns], GROUP, up_ring)
    going_down = lax.ppermute(start[:, chip_columns:], GROUP, down_ring)
    pair = product(1, 3)
    going_up = pair[:rows] + jnp.pad(going_up.astype(f32), ((0, 0), (0, chip_columns)))
    going_down = pair[rows:] + jnp.pad(going_down.astype(f32), ((0, 0), (chip_columns, 0)))
    going_up = lax.ppermute(going_up.astype(bf16), GROUP, up_ring)
    going_down = lax.ppermute(going_down.astype(bf16), GROUP, down_ring)
    for place in (3, 5):
        pair = product(place, place + 2)
        going_up = lax.ppermute((pair[:rows] + going_up.astype(f32)).astype(bf16), GROUP, up_ring)
        going_down = lax.ppermute((pair[rows:] + going_down.astype(f32)).astype(bf16), GROUP, down_ring)
    projected = product(groups - 1, groups) + going_up.astype(f32) + going_down.astype(f32)

    def mine(values, ids_of_rows):
        first = jnp.where(ids_of_rows == my_tenants[0], values[: 2 * rank], 0.0)
        return first, jnp.where(ids_of_rows == my_tenants[1], values[2 * rank :], 0.0)

    flat_ids = row_ids.reshape(1, groups * rows)
    low_parts = sum(mine(contract(inner, token_rows, 1, 1), flat_ids))
    low_parts = low_parts.reshape(2 * rank, groups, rows).transpose(1, 0, 2)
    low_parts = jnp.take(low_parts, place_at, axis=0)
    low_here = lax.all_to_all(low_parts, GROUP, split_axis=0, concat_axis=0, tiled=True)
    low_here = jnp.sum(low_here, axis=0).astype(bf16)
    low = jnp.sum(spread(low_here, CHIPS, chips).astype(f32), axis=0)

    here = row_ids[groups - 1]
    member_of = lax.broadcasted_iota(jnp.int32, (1, 2 * rank, 1), 1) // rank
    delta = 0.0
    for tenants, table in zip(outer_tenants, outers):
        chosen = (tenants[:, None, None] == here[None, None, :])
        placed = [
            jnp.where(chosen & (member_of == member), low[None], 0.0) for member in range(2)
        ]
        placed = jnp.concatenate(placed, axis=2).reshape(chips * 2 * rank, 2 * rows).astype(bf16)
        delta = delta + contract(placed, table, 0, 0)
    gate = projected[:, :chip_columns] + adapter_scale * delta[:rows]
    up = projected[:, chip_columns:] + adapter_scale * delta[rows:]
    sigmoid = jax.nn.sigmoid(gate)
    silu = gate * sigmoid
    hidden_rows = (silu * up).astype(bf16)
    upstream = upstream.astype(f32)
    grad_gate = (upstream * up * sigmoid * (1.0 + gate * (1.0 - sigmoid))).astype(bf16)
    grad_up = (upstream * silu).astype(bf16)
    grads = jnp.concatenate([grad_gate, grad_up], axis=1)

    halves = hidden_rows.reshape(chips, own_rows, 2, columns)
    keep = lax.dynamic_index_in_dim(halves, c, 2, keepdims=False)
    give = lax.dynamic_index_in_dim(halves, 1 - c, 2, keepdims=False)
    hidden = jnp.stack(both(keep, other_core(give)), axis=1).reshape(chips * 2 * own_rows, columns)

    grad_low = []
    for member, grad in enumerate((grad_gate, grad_up)):
        total = 0.0
        for tenants, table in zip(outer_tenants, outers):
            mapped = contract(table, grad, 1, 1).reshape(chips, 2, rank, rows)[:, member]
            total = total + jnp.sum(
                jnp.where(tenants[:, None, None] == here[None, None, :], mapped, 0.0), axis=0
            )
        grad_low.append(total)
    grad_low = (adapter_scale * jnp.concatenate(grad_low, axis=0)).astype(bf16)
    grad_low = jnp.sum(spread(grad_low, CHIPS, chips).astype(f32), axis=0)
    lows = jnp.concatenate([low, grad_low], axis=0).astype(bf16)
    lows = jnp.take(spread(lows, GROUP, groups), group_at, axis=0)
    lows = lows.transpose(1, 0, 2).reshape(4 * rank, groups * rows)
    all_low, all_grad_low = lows[: 2 * rank], lows[2 * rank :]
    own_grad_low = jnp.concatenate(
        mine(jnp.concatenate([all_grad_low, all_grad_low], axis=0), flat_ids), axis=0
    ).astype(bf16)

    grads_at = {0: grads}
    below = lax.ppermute(grads, GROUP, up_ring)
    above = lax.ppermute(grads, GROUP, down_ring)
    grads_at[7], grads_at[1] = below, above
    for step in (2, 3):
        below = lax.ppermute(below, GROUP, up_ring)
        above = lax.ppermute(above, GROUP, down_ring)
        grads_at[groups - step], grads_at[step] = below, above
    far_gate = lax.ppermute(below[:, :chip_columns], GROUP, up_ring)
    far_up = lax.ppermute(above[:, chip_columns:], GROUP, down_ring)
    grads_at[4] = jnp.concatenate([far_gate, far_up], axis=1)

    def back(first, last):
        parts = jnp.concatenate([grads_at[d] for d in ORDER[first:last]], axis=0)
        total = contract(parts, weight, 1, 1)
        return total + contract(own_grad_low[:, first * rows : last * rows], inner, 0, 0)

    def to_owners(first, last):
        part = back(first, last).astype(bf16).reshape(last - first, chips, own_rows, depth)
        part = part.transpose(1, 0, 2, 3).reshape(chips, (last - first) * own_rows, depth)
        got = lax.all_to_all(part, CHIPS, split_axis=0, concat_axis=0, tiled=True)
        return jnp.sum(got.astype(f32), axis=0).astype(bf16)

    near = to_owners(3, 8)
    far = to_owners(0, 3)
    summed = jnp.concatenate([far, near], axis=0).reshape(groups, own_rows, depth)
    summed = jnp.take(summed, place_at, axis=0).reshape(groups * own_rows, depth)
    grad_tokens = lax.all_to_all(summed, GROUP, split_axis=0, concat_axis=1, tiled=True)

    inner_grads = contract(own_grad_low, token_rows, 1, 0)
    grad_in = inner_grads[: 2 * rank] + other_core(inner_grads[2 * rank :])

    all_grads = jnp.concatenate([grads_at[d] for d in ORDER], axis=0)
    share = 2 * chips // groups
    out_tenants = share * z + jnp.arange(share, dtype=jnp.int32)
    chosen = out_tenants[:, None, None] == flat_ids[None]
    outs = []
    for member in range(2):
        placed = jnp.where(chosen, all_low[None, member * rank : (member + 1) * rank], jnp.zeros((), bf16))
        part = contract(
            placed.reshape(share * rank, groups * rows),
            all_grads[:, member * chip_columns : (member + 1) * chip_columns],
            1,
            0,
        )
        outs.append(part.reshape(share // 2, 2, rank, chip_columns))
    outs = jnp.stack(outs, axis=2)
    keep = lax.dynamic_index_in_dim(outs, c, 1, keepdims=False)
    give = lax.dynamic_index_in_dim(outs, 1 - c, 1, keepdims=False)
    outs = (keep + other_core(give.astype(bf16)).astype(f32)).astype(bf16)
    upper, lower = u // 2, u % 2
    same = lax.dynamic_index_in_dim(outs, lower, 0, keepdims=False)
    cross = lax.dynamic_index_in_dim(outs, 1 - lower, 0, keepdims=False)
    straight, crossed = [], []
    for from_z in range(groups):
        for from_u in range(chips):
            h, low_bit = from_u // 2, from_u % 2
            source = from_z * chips + from_u
            straight.append((source, h * chips + 2 * from_z + low_bit))
            crossed.append((source, h * chips + 2 * from_z + 1 - low_bit))
    same = lax.ppermute(same, (GROUP,) + CHIPS, straight)
    cross = lax.ppermute(cross, (GROUP,) + CHIPS, crossed)
    left = jnp.where(lower == 0, same, cross)
    right = jnp.where(lower == 0, cross, same)
    grad_out = adapter_scale * jnp.concatenate([left, right], axis=2).astype(f32)
    return hidden, grad_tokens, grad_in[None], grad_out[None]


def solution(mesh):
    groups, tenants = mesh.shape["dp"], mesh.shape["tenant"]
    split = Mesh(mesh.devices.reshape(groups, tenants // 8, 4, 2), ("z", "y", "x", "c"))
    tenant = ("y", "x", "c")
    in_specs = (
        P(("z",) + tenant, None),
        P("z", tenant),
        P("z", tenant),
        P("z", tenant),
        P(tenant, None, None),
        P(tenant, None, None, None),
        P("z", tenant),
    )
    out_specs = (
        P("z", tenant),
        P(("z",) + tenant, None),
        P(tenant, None, "z"),
        P(tenant, None, None, "z"),
    )
    return jax.shard_map(
        on_device, mesh=split, in_specs=in_specs, out_specs=out_specs, check_vma=False
    )
```

```python
import functools

import jax
import jax.numpy as jnp
from jax import lax
from jax.experimental import pallas as pl
from jax.experimental.pallas import tpu as pltpu
from jax.sharding import Mesh, PartitionSpec as P


adapter_scale = 2.0
bf16 = jnp.bfloat16
f32 = jnp.float32
CHIPS = ("y", "x")
CORE = "c"
GROUP = "z"
ORDER = (4, 3, 5, 2, 6, 1, 7, 0)
LATE = 3


def spread(block, axes, count):
    copies = jnp.broadcast_to(block[None], (count,) + block.shape)
    return lax.all_to_all(copies, axes, split_axis=0, concat_axis=0, tiled=True)


def pick(array, places):
    return array.at[places].get(mode="promise_in_bounds")


WIDE = 512
LIMIT = 12 * 2**20


def dot(a, b, a_dim=1, b_dim=0):
    return lax.dot_general(a, b, (((a_dim,), (b_dim,)), ((), ())), preferred_element_type=f32)


VMEM = pl.BlockSpec(memory_space=pltpu.VMEM)


def call(kernel, info, inputs, outputs, scratch=()):
    return pl.pallas_call(
        kernel,
        out_shape=[jax.ShapeDtypeStruct(shape, dtype) for shape, dtype in outputs],
        in_specs=[pl.BlockSpec(memory_space=pltpu.SMEM)] + [VMEM] * len(inputs),
        out_specs=[VMEM] * len(outputs),
        scratch_shapes=scratch,
        compiler_params=pltpu.CompilerParams(vmem_limit_bytes=LIMIT),
    )(info, *inputs)


def rows_at(tokens, place, own_rows):
    start = place * own_rows
    if not isinstance(place, int):
        start = pl.multiple_of(start, own_rows)
    block = tokens[:, pl.ds(start, own_rows), :]
    return block.reshape(block.shape[0] * own_rows, block.shape[2])


def over_columns(width, body):
    wide = min(WIDE, width)

    def one(step, carry):
        body(pl.ds(pl.multiple_of(step * wide, wide), wide))
        return carry

    lax.fori_loop(0, width // wide, one, 0)


def join_kernel(info, gate, up, other_gate, other_up, hidden, other_hidden, weight, upstream):
    columns = gate.shape[1]
    own = pl.ds(pl.multiple_of(info[2] * columns, columns), columns)
    other = pl.ds(pl.multiple_of((1 - info[2]) * columns, columns), columns)
    weight[0, :, own] = gate[...]
    weight[1, :, own] = up[...]
    weight[0, :, other] = other_gate[...]
    weight[1, :, other] = other_up[...]
    rows = upstream.shape[0]
    upstream[:, own] = hidden[:, info[2]].reshape(rows, columns)
    upstream[:, other] = other_hidden[...].reshape(rows, columns)


def first_kernel(own_rows, info, tokens, weight, gate_out, up_out):
    def body(cols):
        block = rows_at(tokens, 0, own_rows)
        gate_out[:, cols] = dot(block, weight[0, :, cols]).astype(bf16)
        up_out[:, cols] = dot(block, weight[1, :, cols]).astype(bf16)

    over_columns(gate_out.shape[1], body)


def step_kernel(place, own_rows, info, tokens, weight, from_below, from_above, up_out, down_out):
    rows = up_out.shape[1]
    half = from_below.shape[0] == 1

    def body(cols):
        block = jnp.concatenate(
            [rows_at(tokens, place, own_rows), rows_at(tokens, place + 1, own_rows)], axis=0
        )
        for member in range(2):
            product = dot(block, weight[member, :, cols])
            up, down = product[:rows], product[rows:]
            if not half or member == 0:
                up = up + from_below[0 if half else member, :, cols].astype(f32)
            if not half or member == 1:
                down = down + from_above[0 if half else member, :, cols].astype(f32)
            up_out[member, :, cols] = up.astype(bf16)
            down_out[member, :, cols] = down.astype(bf16)

    over_columns(up_out.shape[2], body)


def mine(values, ids, info):
    return jnp.concatenate(
        [jnp.where(ids == info[0], values[0], 0.0), jnp.where(ids == info[1], values[1], 0.0)], axis=0
    )


def low_kernel(own_rows, info, tokens, inner, ids, out):
    def one(place, carry):
        values = dot(inner[...], rows_at(tokens, place, own_rows), 1, 1)
        half = values.shape[0] // 2
        masked = mine((values[:half], values[half:]), ids[pl.ds(place, 1), :], info)
        out[info[4 + place]] = masked[:half] + masked[half:]
        return carry

    lax.fori_loop(0, out.shape[0], one, 0)


def slots_of(shape, ids, info, rank):
    slot = lax.broadcasted_iota(jnp.int32, shape, 0) // rank
    half = shape[0] // rank // 2
    tenant = jnp.where(slot < half, 2 * slot + info[2], 2 * (slot - half) + 1 - info[2])
    return tenant == ids


def middle_kernel(
    rank, own_rows, info, tokens, weight, from_below, from_above, outer, other_outer, low, ids, upstream,
    hidden_out, grads_out, low_out, chosen, mapped,
):
    slots = chosen.shape[2]

    def table(member, cols):
        parts = [ref[:, member, :, cols] for ref in (outer, other_outer)]
        return jnp.concatenate([part.reshape(slots // 2, part.shape[2]) for part in parts], axis=0)

    last = ids.shape[0] - 1
    own = ids[last:, :]
    shape = (slots, own.shape[1])
    here = slots_of(shape, own, info, rank)
    for member in range(2):
        values = low[member * rank : (member + 1) * rank, :].astype(f32)
        values = jnp.concatenate([values] * (slots // rank), axis=0)
        chosen[member] = jnp.where(here, values, 0.0).T.astype(bf16)
    mapped[...] = jnp.zeros_like(mapped)

    def body(cols):
        block = rows_at(tokens, last, own_rows)
        tables = (table(0, cols), table(1, cols))
        gate, up = [
            dot(block, weight[member, :, cols])
            + from_below[member, :, cols].astype(f32)
            + from_above[member, :, cols].astype(f32)
            + adapter_scale * dot(chosen[member], tables[member])
            for member in range(2)
        ]
        cotangent = upstream[:, cols].astype(f32)
        sigmoid = 1.0 / (1.0 + jnp.exp(-gate))
        silu = gate * sigmoid
        hidden_out[:, cols] = (silu * up).astype(bf16)
        grad_gate = (cotangent * up * sigmoid * (1.0 + gate * (1.0 - sigmoid))).astype(bf16)
        grad_up = (cotangent * silu).astype(bf16)
        for member, grad in enumerate((grad_gate, grad_up)):
            grads_out[member, :, cols] = grad
            mapped[member] += dot(tables[member], grad, 1, 1)

    over_columns(hidden_out.shape[1], body)
    here = slots_of(shape, own, info, rank)
    for member in range(2):
        total = jnp.where(here, mapped[member], 0.0).reshape(slots // rank, rank, shape[1])
        low_out[member * rank : (member + 1) * rank, :] = (adapter_scale * jnp.sum(total, axis=0)).astype(bf16)


def grad_low_at(info, lows, ids, place):
    values = lows[info[4 + place], lows.shape[1] // 2 :, :].astype(f32)
    return mine((values, values), ids[place : place + 1, :], info)


def back_kernel(first, count, split, info, weight, inner, lows, ids, *refs):
    *chunks, out, adapters = refs
    pairs = [(ref.at[0], ref.at[1]) for ref in chunks[2 if split else 0 :]]
    chunks = ([(chunks[0], chunks[1])] if split else []) + pairs
    adapter = [grad_low_at(info, lows, ids, first + i).T.astype(bf16) for i in range(count)]
    adapters[...] = jnp.concatenate(adapter, axis=0)
    chips, height, width = out.shape
    deep = min(256, width)
    own_rows, rows = height // count, adapters.shape[0] // count

    def one(step, carry):
        cols = pl.ds(pl.multiple_of(step * deep, deep), deep)
        total = dot(adapters[...], inner[:, cols])
        for member in range(2):
            block = jnp.concatenate([chunk[member][...] for chunk in chunks], axis=0)
            total = total + dot(block, weight[member, cols, :], 1, 1)
        for i in range(count):
            part = total[i * rows : (i + 1) * rows].reshape(chips, own_rows, deep)
            out[:, i * own_rows : (i + 1) * own_rows, cols] = part.astype(bf16)
        return carry

    lax.fori_loop(0, width // deep, one, 0)


def inner_kernel(own_rows, info, tokens, lows, ids, out):
    out[...] = jnp.zeros_like(out)

    def one(place, carry):
        values = lows[info[4 + place], lows.shape[1] // 2 :, :].astype(f32)
        masked = mine((values, values), ids[pl.ds(place, 1), :], info)
        out[...] += dot(masked.astype(bf16), rows_at(tokens, place, own_rows))
        return carry

    lax.fori_loop(0, ids.shape[0], one, 0)


def place_kernel(info, near, far, out):
    own_rows = out.shape[1]
    late = far.shape[1] // own_rows
    for place in range(out.shape[0]):
        if place < late:
            block = far[:, place * own_rows : (place + 1) * own_rows, :].astype(f32)
        else:
            block = near[:, (place - late) * own_rows : (place - late + 1) * own_rows, :].astype(f32)
        out[info[4 + place]] = jnp.sum(block, axis=0).astype(bf16)


def outer_kernel(places, rank, share, split, last, info, lows, ids, *refs):
    refs = list(refs)
    outs = [refs.pop() for _ in range(2 if last else 1)][::-1]
    before = refs.pop() if last else None
    chunks = refs
    if split:
        chunks = [(chunks[0][...], chunks[1][...])] + [(ref[0], ref[1]) for ref in chunks[2:]]
    else:
        chunks = [(ref[0], ref[1]) for ref in chunks]
    rows = chunks[0][0].shape[0]
    slot = lax.broadcasted_iota(jnp.int32, (share * rank, rows), 0) // rank
    half = share // 2
    tenant = share * info[3] + jnp.where(slot < half, 2 * slot + info[2], 2 * (slot - half) + 1 - info[2])
    for member in range(2):
        total = before[member] if last else 0.0
        for place, chunk in zip(places, chunks):
            values = lows[info[4 + place], member * rank : (member + 1) * rank, :].astype(f32)
            values = jnp.concatenate([values] * share, axis=0)
            chosen = jnp.where(tenant == ids[place : place + 1, :], values, 0.0).astype(bf16)
            total = total + dot(chosen, chunk[member])
        if last:
            outs[0][member] = total[: half * rank]
            outs[1][member] = total[half * rank :].astype(bf16)
        else:
            outs[0][member] = total


def on_device(tokens, tenant_ids, gate_weight, up_weight, adapter_in, adapter_out, grad_hidden):
    groups = lax.axis_size(GROUP)
    chips = lax.axis_size("y") * lax.axis_size("x")
    own_rows, _ = tokens.shape
    depth, columns = gate_weight.shape
    rank = adapter_out.shape[2]
    rows = chips * own_rows
    chip_columns = 2 * columns
    z = lax.axis_index(GROUP)
    c = lax.axis_index(CORE)
    u = lax.axis_index("y") * lax.axis_size("x") + lax.axis_index("x")
    first_core = c == 0
    order = jnp.array(ORDER, jnp.int32)
    group_at = (z + order) % groups
    swap = [(0, 1), (1, 0)]
    up_ring = [(i, (i + 1) % groups) for i in range(groups)]
    down_ring = [(i, (i - 1) % groups) for i in range(groups)]

    def other_core(value):
        return lax.ppermute(value, CORE, swap)

    def ring(value, pairs):
        return lax.ppermute(value, GROUP, pairs)

    def both(own, other):
        return jnp.where(first_core, own, other), jnp.where(first_core, other, own)

    ids = jnp.broadcast_to(tenant_ids.reshape(own_rows, 1, 1).astype(bf16), (own_rows, groups, 128))
    wide = jnp.concatenate([tokens.reshape(own_rows, groups, depth), ids], axis=2)
    sliced = lax.all_to_all(
        wide.reshape(own_rows, groups * (depth + 128)), GROUP, split_axis=1, concat_axis=0, tiled=True
    )
    sliced = pick(sliced.reshape(groups, own_rows, depth + 128), group_at)
    sliced = sliced.reshape(groups * own_rows, depth + 128)
    count = groups * own_rows
    id_columns = sliced[:, depth:]
    lane = lax.broadcasted_iota(jnp.int32, (count, 128), 1)
    row = lax.broadcasted_iota(jnp.int32, (count, 128), 0)
    id_lanes = jnp.sum(jnp.where(lane == row, id_columns.astype(f32), 0.0), axis=0, keepdims=True)
    id_block = jnp.broadcast_to(jnp.pad(id_lanes.astype(bf16), ((0, 0), (0, depth - 128))), (8, depth))
    gathered = spread(jnp.concatenate([sliced[:, :depth], id_block], axis=0), CHIPS, chips)
    row_ids = gathered[:, count, :count].astype(f32).astype(jnp.int32)
    row_ids = row_ids.reshape(chips, groups, own_rows).transpose(1, 0, 2).reshape(groups, rows)

    info = jnp.concatenate([jnp.stack([2 * u + c, 2 * u + 1 - c, c, z]), group_at]).astype(jnp.int32)
    by_core = grad_hidden.reshape(chips, 2, own_rows, columns)
    give = lax.dynamic_index_in_dim(by_core, 1 - c, 1, keepdims=False)
    weight, upstream = call(
        join_kernel,
        info,
        [gate_weight, up_weight, other_core(gate_weight), other_core(up_weight), by_core, other_core(give)],
        [((2, depth, chip_columns), bf16), ((rows, chip_columns), bf16)],
    )

    inner = lax.dynamic_slice_in_dim(adapter_in[0], z * depth, depth, axis=1)
    inner = jnp.concatenate([inner, other_core(inner)], axis=0)
    outer = adapter_out.reshape(2 * rank, chips, chip_columns).transpose(1, 0, 2)
    outer = lax.all_to_all(outer, CHIPS, split_axis=0, concat_axis=0, tiled=True)
    outer = outer.reshape(chips, 2, rank, chip_columns)
    other_outer = other_core(outer)

    shape = (rows, chip_columns)
    going_up, going_down = call(
        functools.partial(first_kernel, own_rows), info, [gathered, weight], [(shape, bf16)] * 2
    )
    going_up = ring(going_up, up_ring)[None]
    going_down = ring(going_down, down_ring)[None]
    for step, place in enumerate((1, 3, 5), 2):
        going_up, going_down = call(
            functools.partial(step_kernel, place, own_rows),
            info,
            [gathered, weight, going_up, going_down],
            [((2,) + shape, bf16)] * 2,
        )
        going_up = ring(going_up, up_ring)
        going_down = ring(going_down, down_ring)

    (low_parts,) = call(
        functools.partial(low_kernel, own_rows), info, [gathered, inner, row_ids], [((groups, 2 * rank, rows), f32)]
    )
    low_here = lax.all_to_all(low_parts, GROUP, split_axis=0, concat_axis=0, tiled=True)
    low_here = jnp.sum(low_here, axis=0).astype(bf16)
    low = spread(low_here, CHIPS, chips)
    low = jnp.sum(low.astype(f32), axis=0).astype(bf16)

    slots = 2 * chips * rank
    hidden_rows, grads, grad_low = call(
        functools.partial(middle_kernel, rank, own_rows),
        info,
        [gathered, weight, going_up, going_down, outer, other_outer, low, row_ids, upstream],
        [(shape, bf16), ((2,) + shape, bf16), ((2 * rank, rows), bf16)],
        (pltpu.VMEM((2, rows, slots), bf16), pltpu.VMEM((2, slots, rows), f32)),
    )

    grads_at = {0: [grads]}
    below = ring(grads, up_ring)
    above = ring(grads, down_ring)
    grads_at[7], grads_at[1] = [below], [above]
    for step in (2, 3):
        below = ring(below, up_ring)
        above = ring(above, down_ring)
        grads_at[groups - step], grads_at[step] = [below], [above]
    grads_at[4] = [ring(below[0], up_ring), ring(above[1], down_ring)]

    halves = hidden_rows.reshape(chips, own_rows, 2, columns)
    keep = lax.dynamic_index_in_dim(halves, c, 2, keepdims=False)
    give = lax.dynamic_index_in_dim(halves, 1 - c, 2, keepdims=False)
    hidden = jnp.stack(both(keep, other_core(give)), axis=1).reshape(chips * 2 * own_rows, columns)

    grad_low = spread(grad_low, CHIPS, chips)
    grad_low = jnp.sum(grad_low.astype(f32), axis=0).astype(bf16)
    lows = jnp.concatenate([low, grad_low], axis=0)
    lows = spread(lows, GROUP, groups)

    def to_owners(first, last):
        count = last - first
        chunks = [array for d in ORDER[first:last] for array in grads_at[d]]
        (part,) = call(
            functools.partial(back_kernel, first, count, first == 0),
            info,
            [weight, inner, lows, row_ids] + chunks,
            [((chips, count * own_rows, depth), bf16)],
            (pltpu.VMEM((count * rows, inner.shape[0]), bf16),),
        )
        return lax.all_to_all(part, CHIPS, split_axis=0, concat_axis=0, tiled=True)

    near = to_owners(LATE, groups)
    far = to_owners(0, LATE)
    (summed,) = call(place_kernel, info, [near, far], [((groups, own_rows, depth), bf16)])
    grad_tokens = lax.all_to_all(
        summed.reshape(groups * own_rows, depth), GROUP, split_axis=0, concat_axis=1, tiled=True
    )

    (inner_grads,) = call(
        functools.partial(inner_kernel, own_rows), info, [gathered, lows, row_ids], [((4 * rank, depth), f32)]
    )
    grad_in = inner_grads[: 2 * rank] + other_core(inner_grads[2 * rank :])

    share = 2 * chips // groups

    def outer_grads(places, before):
        chunks = [array for place in places for array in grads_at[ORDER[place]]]
        arrays = [lows, row_ids] + chunks + ([] if before is None else [before])
        full = (2, share * rank, chip_columns)
        part = (2, share // 2 * rank, chip_columns)
        outs = [(full, f32)] if before is None else [(part, f32), (part, bf16)]
        return call(
            functools.partial(outer_kernel, places, rank, share, 0 in places, before is not None), info, arrays, outs
        )

    (outs,) = outer_grads(tuple(range(LATE, groups)), None)
    keep, give = outer_grads(tuple(range(LATE)), outs)
    outs = (keep + other_core(give).astype(f32)).astype(bf16)
    outs = outs.reshape(2, share // 2, rank, chip_columns)
    lower = u % 2
    same = lax.dynamic_index_in_dim(outs, lower, 1, keepdims=False)
    cross = lax.dynamic_index_in_dim(outs, 1 - lower, 1, keepdims=False)
    straight, crossed = [], []
    for from_z in range(groups):
        for from_u in range(chips):
            source, low_bit = from_z * chips + from_u, from_u % 2
            target = (from_u // 2) * chips + 2 * from_z
            straight.append((source, target + low_bit))
            crossed.append((source, target + 1 - low_bit))
    same = lax.ppermute(same, (GROUP,) + CHIPS, straight)
    cross = lax.ppermute(cross, (GROUP,) + CHIPS, crossed)
    left = jnp.where(lower == 0, same, cross)
    right = jnp.where(lower == 0, cross, same)
    grad_out = adapter_scale * jnp.concatenate([left, right], axis=2).astype(f32)
    return hidden, grad_tokens, grad_in[None], grad_out[None]


def solution(mesh):
    groups, tenants = mesh.shape["dp"], mesh.shape["tenant"]
    split = Mesh(mesh.devices.reshape(groups, tenants // 8, 4, 2), ("z", "y", "x", "c"))
    tenant = ("y", "x", "c")
    in_specs = (
        P(("z",) + tenant, None),
        P("z", tenant),
        P("z", tenant),
        P("z", tenant),
        P(tenant, None, None),
        P(tenant, None, None, None),
        P("z", tenant),
    )
    out_specs = (
        P("z", tenant),
        P(("z",) + tenant, None),
        P(tenant, None, "z"),
        P(tenant, None, None, "z"),
    )
    return jax.shard_map(on_device, mesh=split, in_specs=in_specs, out_specs=out_specs, check_vma=False)
```

```python
import functools

import jax
import jax.numpy as jnp
from jax import lax
from jax.experimental import pallas as pl
from jax.experimental.pallas import tpu as pltpu
from jax.sharding import Mesh, PartitionSpec as P


adapter_scale = 2.0
bf16 = jnp.bfloat16
f32 = jnp.float32
CHIPS = ("y", "x")
CORE = "c"
GROUP = "z"
ORDER = (4, 3, 5, 2, 6, 1, 7, 0)
LATE = 3


def spread(block, axes, count):
    copies = jnp.broadcast_to(block[None], (count,) + block.shape)
    return lax.all_to_all(copies, axes, split_axis=0, concat_axis=0, tiled=True)


def pick(array, places):
    return array.at[places].get(mode="promise_in_bounds")


WIDE = 512
LIMIT = 12 * 2**20


def dot(a, b, a_dim=1, b_dim=0):
    return lax.dot_general(a, b, (((a_dim,), (b_dim,)), ((), ())), preferred_element_type=f32)


VMEM = pl.BlockSpec(memory_space=pltpu.VMEM)


def call(kernel, info, inputs, outputs, scratch=()):
    return pl.pallas_call(
        kernel,
        out_shape=[jax.ShapeDtypeStruct(shape, dtype) for shape, dtype in outputs],
        in_specs=[pl.BlockSpec(memory_space=pltpu.SMEM)] + [VMEM] * len(inputs),
        out_specs=[VMEM] * len(outputs),
        scratch_shapes=scratch,
        compiler_params=pltpu.CompilerParams(vmem_limit_bytes=LIMIT),
    )(info, *inputs)


def rows_at(tokens, place, own_rows):
    start = place * own_rows
    if not isinstance(place, int):
        start = pl.multiple_of(start, own_rows)
    block = tokens[:, pl.ds(start, own_rows), :]
    return block.reshape(block.shape[0] * own_rows, block.shape[2])


def over_columns(width, body):
    wide = min(WIDE, width)

    def one(step, carry):
        body(pl.ds(pl.multiple_of(step * wide, wide), wide))
        return carry

    lax.fori_loop(0, width // wide, one, 0)


def join_kernel(info, gate, up, other_gate, other_up, hidden, other_hidden, weight, upstream):
    columns = gate.shape[1]
    own = pl.ds(pl.multiple_of(info[2] * columns, columns), columns)
    other = pl.ds(pl.multiple_of((1 - info[2]) * columns, columns), columns)
    weight[0, :, own] = gate[...]
    weight[1, :, own] = up[...]
    weight[0, :, other] = other_gate[...]
    weight[1, :, other] = other_up[...]
    rows = upstream.shape[0]
    upstream[:, own] = hidden[:, info[2]].reshape(rows, columns)
    upstream[:, other] = other_hidden[...].reshape(rows, columns)


def first_kernel(own_rows, info, tokens, weight, gate_out, up_out):
    def body(cols):
        block = rows_at(tokens, 0, own_rows)
        gate_out[:, cols] = dot(block, weight[0, :, cols]).astype(bf16)
        up_out[:, cols] = dot(block, weight[1, :, cols]).astype(bf16)

    over_columns(gate_out.shape[1], body)


def rest_kernel(own_rows, info, tokens, weight, *outs):
    rows = outs[0].shape[2]
    held = [(out, i) for out in outs for i in range(out.shape[0])]

    def body(cols):
        block = jnp.concatenate(
            [rows_at(tokens, place, own_rows) for place in range(1, len(held) + 1)], axis=0
        )
        for member in range(2):
            product = dot(block, weight[member, :, cols]).astype(bf16)
            for at, (out, i) in enumerate(held):
                out[i, member, :, cols] = product[at * rows : (at + 1) * rows]

    over_columns(outs[0].shape[3], body)


def mine(values, ids, info):
    return jnp.concatenate(
        [jnp.where(ids == info[0], values[0], 0.0), jnp.where(ids == info[1], values[1], 0.0)], axis=0
    )


def low_kernel(own_rows, info, tokens, inner, ids, out):
    def one(place, carry):
        values = dot(inner[...], rows_at(tokens, place, own_rows), 1, 1)
        half = values.shape[0] // 2
        masked = mine((values[:half], values[half:]), ids[pl.ds(place, 1), :], info)
        out[info[4 + place]] = masked[:half] + masked[half:]
        return carry

    lax.fori_loop(0, out.shape[0], one, 0)


def slots_of(shape, ids, info, rank):
    slot = lax.broadcasted_iota(jnp.int32, shape, 0) // rank
    half = shape[0] // rank // 2
    tenant = jnp.where(slot < half, 2 * slot + info[2], 2 * (slot - half) + 1 - info[2])
    return tenant == ids


def middle_kernel(
    rank, info, product, from_below, from_above, outer, other_outer, low, ids, upstream,
    hidden_out, grads_out, low_out, chosen, mapped,
):
    slots = chosen.shape[2]

    def table(member, cols):
        parts = [ref[:, member, :, cols] for ref in (outer, other_outer)]
        return jnp.concatenate([part.reshape(slots // 2, part.shape[2]) for part in parts], axis=0)

    last = ids.shape[0] - 1
    own = ids[last:, :]
    shape = (slots, own.shape[1])
    here = slots_of(shape, own, info, rank)
    for member in range(2):
        values = low[member * rank : (member + 1) * rank, :].astype(f32)
        values = jnp.concatenate([values] * (slots // rank), axis=0)
        chosen[member] = jnp.where(here, values, 0.0).T.astype(bf16)
    mapped[...] = jnp.zeros_like(mapped)

    def body(cols):
        tables = (table(0, cols), table(1, cols))
        gate, up = [
            product[0, member, :, cols].astype(f32)
            + from_below[member, :, cols].astype(f32)
            + from_above[member, :, cols].astype(f32)
            + adapter_scale * dot(chosen[member], tables[member])
            for member in range(2)
        ]
        cotangent = upstream[:, cols].astype(f32)
        sigmoid = 1.0 / (1.0 + jnp.exp(-gate))
        silu = gate * sigmoid
        hidden_out[:, cols] = (silu * up).astype(bf16)
        grad_gate = (cotangent * up * sigmoid * (1.0 + gate * (1.0 - sigmoid))).astype(bf16)
        grad_up = (cotangent * silu).astype(bf16)
        for member, grad in enumerate((grad_gate, grad_up)):
            grads_out[member, :, cols] = grad
            mapped[member] += dot(tables[member], grad, 1, 1)

    over_columns(hidden_out.shape[1], body)
    here = slots_of(shape, own, info, rank)
    for member in range(2):
        total = jnp.where(here, mapped[member], 0.0).reshape(slots // rank, rank, shape[1])
        low_out[member * rank : (member + 1) * rank, :] = (adapter_scale * jnp.sum(total, axis=0)).astype(bf16)


def grad_low_at(info, lows, ids, place):
    values = lows[info[4 + place], lows.shape[1] // 2 :, :].astype(f32)
    return mine((values, values), ids[place : place + 1, :], info)


def back_kernel(first, count, split, info, weight, inner, lows, ids, *refs):
    *chunks, out, adapters = refs
    pairs = [(ref.at[0], ref.at[1]) for ref in chunks[2 if split else 0 :]]
    chunks = ([(chunks[0], chunks[1])] if split else []) + pairs
    adapter = [grad_low_at(info, lows, ids, first + i).T.astype(bf16) for i in range(count)]
    adapters[...] = jnp.concatenate(adapter, axis=0)
    chips, height, width = out.shape
    deep = min(256, width)
    own_rows, rows = height // count, adapters.shape[0] // count

    def one(step, carry):
        cols = pl.ds(pl.multiple_of(step * deep, deep), deep)
        total = dot(adapters[...], inner[:, cols])
        for member in range(2):
            block = jnp.concatenate([chunk[member][...] for chunk in chunks], axis=0)
            total = total + dot(block, weight[member, cols, :], 1, 1)
        for i in range(count):
            part = total[i * rows : (i + 1) * rows].reshape(chips, own_rows, deep)
            out[:, i * own_rows : (i + 1) * own_rows, cols] = part.astype(bf16)
        return carry

    lax.fori_loop(0, width // deep, one, 0)


def inner_kernel(own_rows, info, tokens, lows, ids, out):
    out[...] = jnp.zeros_like(out)

    def one(place, carry):
        values = lows[info[4 + place], lows.shape[1] // 2 :, :].astype(f32)
        masked = mine((values, values), ids[pl.ds(place, 1), :], info)
        out[...] += dot(masked.astype(bf16), rows_at(tokens, place, own_rows))
        return carry

    lax.fori_loop(0, ids.shape[0], one, 0)


def place_kernel(info, near, far, out):
    own_rows = out.shape[1]
    late = far.shape[1] // own_rows
    for place in range(out.shape[0]):
        if place < late:
            block = far[:, place * own_rows : (place + 1) * own_rows, :].astype(f32)
        else:
            block = near[:, (place - late) * own_rows : (place - late + 1) * own_rows, :].astype(f32)
        out[info[4 + place]] = jnp.sum(block, axis=0).astype(bf16)


def outer_kernel(places, rank, share, split, last, info, lows, ids, *refs):
    refs = list(refs)
    outs = [refs.pop() for _ in range(2 if last else 1)][::-1]
    before = refs.pop() if last else None
    chunks = refs
    if split:
        chunks = [(chunks[0][...], chunks[1][...])] + [(ref[0], ref[1]) for ref in chunks[2:]]
    else:
        chunks = [(ref[0], ref[1]) for ref in chunks]
    rows = chunks[0][0].shape[0]
    slot = lax.broadcasted_iota(jnp.int32, (share * rank, rows), 0) // rank
    half = share // 2
    tenant = share * info[3] + jnp.where(slot < half, 2 * slot + info[2], 2 * (slot - half) + 1 - info[2])
    for member in range(2):
        total = before[member] if last else 0.0
        for place, chunk in zip(places, chunks):
            values = lows[info[4 + place], member * rank : (member + 1) * rank, :].astype(f32)
            values = jnp.concatenate([values] * share, axis=0)
            chosen = jnp.where(tenant == ids[place : place + 1, :], values, 0.0).astype(bf16)
            total = total + dot(chosen, chunk[member])
        if last:
            outs[0][member] = total[: half * rank]
            outs[1][member] = total[half * rank :].astype(bf16)
        else:
            outs[0][member] = total


def on_device(tokens, tenant_ids, gate_weight, up_weight, adapter_in, adapter_out, grad_hidden):
    groups = lax.axis_size(GROUP)
    chips = lax.axis_size("y") * lax.axis_size("x")
    own_rows, _ = tokens.shape
    depth, columns = gate_weight.shape
    rank = adapter_out.shape[2]
    rows = chips * own_rows
    chip_columns = 2 * columns
    z = lax.axis_index(GROUP)
    c = lax.axis_index(CORE)
    u = lax.axis_index("y") * lax.axis_size("x") + lax.axis_index("x")
    first_core = c == 0
    order = jnp.array(ORDER, jnp.int32)
    group_at = (z + order) % groups
    swap = [(0, 1), (1, 0)]
    up_ring = [(i, (i + 1) % groups) for i in range(groups)]
    down_ring = [(i, (i - 1) % groups) for i in range(groups)]

    def other_core(value):
        return lax.ppermute(value, CORE, swap)

    def ring(value, pairs):
        return lax.ppermute(value, GROUP, pairs)

    def both(own, other):
        return jnp.where(first_core, own, other), jnp.where(first_core, other, own)

    ids = jnp.broadcast_to(tenant_ids.reshape(own_rows, 1, 1).astype(bf16), (own_rows, groups, 128))
    wide = jnp.concatenate([tokens.reshape(own_rows, groups, depth), ids], axis=2)
    sliced = lax.all_to_all(
        wide.reshape(own_rows, groups * (depth + 128)), GROUP, split_axis=1, concat_axis=0, tiled=True
    )
    sliced = pick(sliced.reshape(groups, own_rows, depth + 128), group_at)
    sliced = sliced.reshape(groups * own_rows, depth + 128)
    count = groups * own_rows
    id_columns = sliced[:, depth:]
    lane = lax.broadcasted_iota(jnp.int32, (count, 128), 1)
    row = lax.broadcasted_iota(jnp.int32, (count, 128), 0)
    id_lanes = jnp.sum(jnp.where(lane == row, id_columns.astype(f32), 0.0), axis=0, keepdims=True)
    id_block = jnp.broadcast_to(jnp.pad(id_lanes.astype(bf16), ((0, 0), (0, depth - 128))), (8, depth))
    gathered = spread(jnp.concatenate([sliced[:, :depth], id_block], axis=0), CHIPS, chips)
    row_ids = gathered[:, count, :count].astype(f32).astype(jnp.int32)
    row_ids = row_ids.reshape(chips, groups, own_rows).transpose(1, 0, 2).reshape(groups, rows)

    info = jnp.concatenate([jnp.stack([2 * u + c, 2 * u + 1 - c, c, z]), group_at]).astype(jnp.int32)
    by_core = grad_hidden.reshape(chips, 2, own_rows, columns)
    give = lax.dynamic_index_in_dim(by_core, 1 - c, 1, keepdims=False)
    weight, upstream = call(
        join_kernel,
        info,
        [gate_weight, up_weight, other_core(gate_weight), other_core(up_weight), by_core, other_core(give)],
        [((2, depth, chip_columns), bf16), ((rows, chip_columns), bf16)],
    )

    inner = lax.dynamic_slice_in_dim(adapter_in[0], z * depth, depth, axis=1)
    inner = jnp.concatenate([inner, other_core(inner)], axis=0)
    outer = adapter_out.reshape(2 * rank, chips, chip_columns).transpose(1, 0, 2)
    outer = lax.all_to_all(outer, CHIPS, split_axis=0, concat_axis=0, tiled=True)
    outer = outer.reshape(chips, 2, rank, chip_columns)
    other_outer = other_core(outer)

    shape = (rows, chip_columns)
    going_up, going_down = call(
        functools.partial(first_kernel, own_rows), info, [gathered, weight], [(shape, bf16)] * 2
    )
    going_up = ring(going_up, up_ring)[None]
    going_down = ring(going_down, down_ring)[None]
    going_up = jnp.pad(going_up, ((0, 1), (0, 0), (0, 0)))
    going_down = jnp.pad(going_down, ((1, 0), (0, 0), (0, 0)))
    *pairs, product = call(
        functools.partial(rest_kernel, own_rows),
        info,
        [gathered, weight],
        [((count, 2) + shape, bf16) for count in (2, 2, 2, 1)],
    )
    for step, pair in enumerate(pairs, 2):
        going_up = (pair[0].astype(f32) + going_up.astype(f32)).astype(bf16)
        going_down = (pair[1].astype(f32) + going_down.astype(f32)).astype(bf16)
        going_up = ring(going_up, up_ring)
        going_down = ring(going_down, down_ring)

    (low_parts,) = call(
        functools.partial(low_kernel, own_rows), info, [gathered, inner, row_ids], [((groups, 2 * rank, rows), f32)]
    )
    low_here = lax.all_to_all(low_parts, GROUP, split_axis=0, concat_axis=0, tiled=True)
    low_here = jnp.sum(low_here, axis=0).astype(bf16)
    low = spread(low_here, CHIPS, chips)
    low = jnp.sum(low.astype(f32), axis=0).astype(bf16)

    slots = 2 * chips * rank
    hidden_rows, grads, grad_low = call(
        functools.partial(middle_kernel, rank),
        info,
        [product, going_up, going_down, outer, other_outer, low, row_ids, upstream],
        [(shape, bf16), ((2,) + shape, bf16), ((2 * rank, rows), bf16)],
        (pltpu.VMEM((2, rows, slots), bf16), pltpu.VMEM((2, slots, rows), f32)),
    )

    grads_at = {0: [grads]}
    below = ring(grads, up_ring)
    above = ring(grads, down_ring)
    grads_at[7], grads_at[1] = [below], [above]
    for step in (2, 3):
        below = ring(below, up_ring)
        above = ring(above, down_ring)
        grads_at[groups - step], grads_at[step] = [below], [above]
    grads_at[4] = [ring(below[0], up_ring), ring(above[1], down_ring)]

    halves = hidden_rows.reshape(chips, own_rows, 2, columns)
    keep = lax.dynamic_index_in_dim(halves, c, 2, keepdims=False)
    give = lax.dynamic_index_in_dim(halves, 1 - c, 2, keepdims=False)
    hidden = jnp.stack(both(keep, other_core(give)), axis=1).reshape(chips * 2 * own_rows, columns)

    grad_low = spread(grad_low, CHIPS, chips)
    grad_low = jnp.sum(grad_low.astype(f32), axis=0).astype(bf16)
    lows = jnp.concatenate([low, grad_low], axis=0)
    lows = spread(lows, GROUP, groups)

    def to_owners(first, last):
        count = last - first
        chunks = [array for d in ORDER[first:last] for array in grads_at[d]]
        (part,) = call(
            functools.partial(back_kernel, first, count, first == 0),
            info,
            [weight, inner, lows, row_ids] + chunks,
            [((chips, count * own_rows, depth), bf16)],
            (pltpu.VMEM((count * rows, inner.shape[0]), bf16),),
        )
        return lax.all_to_all(part, CHIPS, split_axis=0, concat_axis=0, tiled=True)

    near = to_owners(LATE, groups)
    far = to_owners(0, LATE)
    (summed,) = call(place_kernel, info, [near, far], [((groups, own_rows, depth), bf16)])
    grad_tokens = lax.all_to_all(
        summed.reshape(groups * own_rows, depth), GROUP, split_axis=0, concat_axis=1, tiled=True
    )

    (inner_grads,) = call(
        functools.partial(inner_kernel, own_rows), info, [gathered, lows, row_ids], [((4 * rank, depth), f32)]
    )
    grad_in = inner_grads[: 2 * rank] + other_core(inner_grads[2 * rank :])

    share = 2 * chips // groups

    def outer_grads(places, before):
        chunks = [array for place in places for array in grads_at[ORDER[place]]]
        arrays = [lows, row_ids] + chunks + ([] if before is None else [before])
        full = (2, share * rank, chip_columns)
        part = (2, share // 2 * rank, chip_columns)
        outs = [(full, f32)] if before is None else [(part, f32), (part, bf16)]
        return call(
            functools.partial(outer_kernel, places, rank, share, 0 in places, before is not None), info, arrays, outs
        )

    (outs,) = outer_grads(tuple(range(LATE, groups)), None)
    keep, give = outer_grads(tuple(range(LATE)), outs)
    outs = (keep + other_core(give).astype(f32)).astype(bf16)
    outs = outs.reshape(2, share // 2, rank, chip_columns)
    lower = u % 2
    same = lax.dynamic_index_in_dim(outs, lower, 1, keepdims=False)
    cross = lax.dynamic_index_in_dim(outs, 1 - lower, 1, keepdims=False)
    straight, crossed = [], []
    for from_z in range(groups):
        for from_u in range(chips):
            source, low_bit = from_z * chips + from_u, from_u % 2
            target = (from_u // 2) * chips + 2 * from_z
            straight.append((source, target + low_bit))
            crossed.append((source, target + 1 - low_bit))
    same = lax.ppermute(same, (GROUP,) + CHIPS, straight)
    cross = lax.ppermute(cross, (GROUP,) + CHIPS, crossed)
    left = jnp.where(lower == 0, same, cross)
    right = jnp.where(lower == 0, cross, same)
    grad_out = adapter_scale * jnp.concatenate([left, right], axis=2).astype(f32)
    return hidden, grad_tokens, grad_in[None], grad_out[None]


def solution(mesh):
    groups, tenants = mesh.shape["dp"], mesh.shape["tenant"]
    split = Mesh(mesh.devices.reshape(groups, tenants // 8, 4, 2), ("z", "y", "x", "c"))
    tenant = ("y", "x", "c")
    in_specs = (
        P(("z",) + tenant, None),
        P("z", tenant),
        P("z", tenant),
        P("z", tenant),
        P(tenant, None, None),
        P(tenant, None, None, None),
        P("z", tenant),
    )
    out_specs = (
        P("z", tenant),
        P(("z",) + tenant, None),
        P(tenant, None, "z"),
        P(tenant, None, None, "z"),
    )
    return jax.shard_map(on_device, mesh=split, in_specs=in_specs, out_specs=out_specs, check_vma=False)
```

```python
import functools

import jax
import jax.numpy as jnp
from jax import lax
from jax.experimental import pallas as pl
from jax.experimental.pallas import tpu as pltpu
from jax.sharding import Mesh, PartitionSpec as P


adapter_scale = 2.0
bf16 = jnp.bfloat16
f32 = jnp.float32
CHIPS = ("y", "x")
CORE = "c"
GROUP = "z"
ORDER = (4, 3, 5, 2, 6, 1, 7, 0)
LATE = 3


def spread(block, axes, count):
    copies = jnp.broadcast_to(block[None], (count,) + block.shape)
    return lax.all_to_all(copies, axes, split_axis=0, concat_axis=0, tiled=True)


def pick(array, places):
    return array.at[places].get(mode="promise_in_bounds")


WIDE = 512
LIMIT = 12 * 2**20


def dot(a, b, a_dim=1, b_dim=0):
    return lax.dot_general(a, b, (((a_dim,), (b_dim,)), ((), ())), preferred_element_type=f32)


VMEM = pl.BlockSpec(memory_space=pltpu.VMEM)


def call(kernel, info, inputs, outputs, scratch=()):
    return pl.pallas_call(
        kernel,
        out_shape=[jax.ShapeDtypeStruct(shape, dtype) for shape, dtype in outputs],
        in_specs=[pl.BlockSpec(memory_space=pltpu.SMEM)] + [VMEM] * len(inputs),
        out_specs=[VMEM] * len(outputs),
        scratch_shapes=scratch,
        compiler_params=pltpu.CompilerParams(vmem_limit_bytes=LIMIT),
    )(info, *inputs)


def rows_at(tokens, place, own_rows):
    parts = (tokens.shape[1] - 8) // (8 * own_rows)
    blocks = []
    for part in range(parts):
        start = (place * parts + part) * own_rows
        if not isinstance(place, int):
            start = pl.multiple_of(start, own_rows)
        block = tokens[:, pl.ds(start, own_rows), :]
        blocks.append(block.reshape(block.shape[0] * own_rows, block.shape[2]))
    return jnp.concatenate(blocks, axis=1)


def over_columns(width, body):
    wide = min(WIDE, width)

    def one(step, carry):
        body(pl.ds(pl.multiple_of(step * wide, wide), wide))
        return carry

    lax.fori_loop(0, width // wide, one, 0)


def join_kernel(info, gate, up, other_gate, other_up, hidden, other_hidden, weight, upstream):
    columns = gate.shape[1]
    own = pl.ds(pl.multiple_of(info[2] * columns, columns), columns)
    other = pl.ds(pl.multiple_of((1 - info[2]) * columns, columns), columns)
    weight[0, :, own] = gate[...]
    weight[1, :, own] = up[...]
    weight[0, :, other] = other_gate[...]
    weight[1, :, other] = other_up[...]
    rows = upstream.shape[0]
    upstream[:, own] = hidden[:, info[2]].reshape(rows, columns)
    upstream[:, other] = other_hidden[...].reshape(rows, columns)


def first_kernel(own_rows, info, tokens, weight, gate_out, up_out):
    def body(cols):
        block = rows_at(tokens, 0, own_rows)
        gate_out[:, cols] = dot(block, weight[0, :, cols]).astype(bf16)
        up_out[:, cols] = dot(block, weight[1, :, cols]).astype(bf16)

    over_columns(gate_out.shape[1], body)


def rest_kernel(own_rows, info, tokens, weight, *outs):
    rows = outs[0].shape[2]
    held = [(out, i) for out in outs for i in range(out.shape[0])]

    def body(cols):
        block = jnp.concatenate(
            [rows_at(tokens, place, own_rows) for place in range(1, len(held) + 1)], axis=0
        )
        for member in range(2):
            product = dot(block, weight[member, :, cols]).astype(bf16)
            for at, (out, i) in enumerate(held):
                out[i, member, :, cols] = product[at * rows : (at + 1) * rows]

    over_columns(outs[0].shape[3], body)


def mine(values, ids, info):
    return jnp.concatenate(
        [jnp.where(ids == info[0], values[0], 0.0), jnp.where(ids == info[1], values[1], 0.0)], axis=0
    )


def low_kernel(own_rows, info, tokens, inner, ids, out):
    def one(place, carry):
        values = dot(inner[...], rows_at(tokens, place, own_rows), 1, 1)
        half = values.shape[0] // 2
        masked = mine((values[:half], values[half:]), ids[pl.ds(place, 1), :], info)
        out[info[4 + place]] = masked[:half] + masked[half:]
        return carry

    lax.fori_loop(0, out.shape[0], one, 0)


def slots_of(shape, ids, info, rank):
    slot = lax.broadcasted_iota(jnp.int32, shape, 0) // rank
    half = shape[0] // rank // 2
    tenant = jnp.where(slot < half, 2 * slot + info[2], 2 * (slot - half) + 1 - info[2])
    return tenant == ids


def middle_kernel(
    rank, info, product, from_below, from_above, outer, other_outer, low, ids, upstream,
    hidden_out, grads_out, low_out, chosen, mapped,
):
    slots = chosen.shape[2]

    def table(member, cols):
        parts = [ref[:, member, :, cols] for ref in (outer, other_outer)]
        return jnp.concatenate([part.reshape(slots // 2, part.shape[2]) for part in parts], axis=0)

    last = ids.shape[0] - 1
    own = ids[last:, :]
    shape = (slots, own.shape[1])
    here = slots_of(shape, own, info, rank)
    for member in range(2):
        values = low[member * rank : (member + 1) * rank, :].astype(f32)
        values = jnp.concatenate([values] * (slots // rank), axis=0)
        chosen[member] = jnp.where(here, values, 0.0).T.astype(bf16)
    mapped[...] = jnp.zeros_like(mapped)

    def body(cols):
        tables = (table(0, cols), table(1, cols))
        gate, up = [
            product[0, member, :, cols].astype(f32)
            + from_below[member, :, cols].astype(f32)
            + from_above[member, :, cols].astype(f32)
            + adapter_scale * dot(chosen[member], tables[member])
            for member in range(2)
        ]
        cotangent = upstream[:, cols].astype(f32)
        sigmoid = 1.0 / (1.0 + jnp.exp(-gate))
        silu = gate * sigmoid
        hidden_out[:, cols] = (silu * up).astype(bf16)
        grad_gate = (cotangent * up * sigmoid * (1.0 + gate * (1.0 - sigmoid))).astype(bf16)
        grad_up = (cotangent * silu).astype(bf16)
        for member, grad in enumerate((grad_gate, grad_up)):
            grads_out[member, :, cols] = grad
            mapped[member] += dot(tables[member], grad, 1, 1)

    over_columns(hidden_out.shape[1], body)
    here = slots_of(shape, own, info, rank)
    for member in range(2):
        total = jnp.where(here, mapped[member], 0.0).reshape(slots // rank, rank, shape[1])
        low_out[member * rank : (member + 1) * rank, :] = (adapter_scale * jnp.sum(total, axis=0)).astype(bf16)


def grad_low_at(info, lows, ids, place):
    values = lows[info[4 + place], lows.shape[1] // 2 :, :].astype(f32)
    return mine((values, values), ids[place : place + 1, :], info)


def back_kernel(first, count, split, info, weight, inner, lows, ids, *refs):
    *chunks, out, adapters = refs
    pairs = [(ref.at[0], ref.at[1]) for ref in chunks[2 if split else 0 :]]
    chunks = ([(chunks[0], chunks[1])] if split else []) + pairs
    adapter = [grad_low_at(info, lows, ids, first + i).T.astype(bf16) for i in range(count)]
    adapters[...] = jnp.concatenate(adapter, axis=0)
    chips, height, width = out.shape
    deep = min(256, width)
    own_rows, rows = height // count, adapters.shape[0] // count

    def one(step, carry):
        cols = pl.ds(pl.multiple_of(step * deep, deep), deep)
        total = dot(adapters[...], inner[:, cols])
        for member in range(2):
            block = jnp.concatenate([chunk[member][...] for chunk in chunks], axis=0)
            total = total + dot(block, weight[member, cols, :], 1, 1)
        for i in range(count):
            part = total[i * rows : (i + 1) * rows].reshape(chips, own_rows, deep)
            out[:, i * own_rows : (i + 1) * own_rows, cols] = part.astype(bf16)
        return carry

    lax.fori_loop(0, width // deep, one, 0)


def inner_kernel(own_rows, info, tokens, lows, ids, out):
    out[...] = jnp.zeros_like(out)

    def one(place, carry):
        values = lows[info[4 + place], lows.shape[1] // 2 :, :].astype(f32)
        masked = mine((values, values), ids[pl.ds(place, 1), :], info)
        out[...] += dot(masked.astype(bf16), rows_at(tokens, place, own_rows))
        return carry

    lax.fori_loop(0, ids.shape[0], one, 0)


def place_kernel(info, near, far, out):
    own_rows = out.shape[1]
    late = far.shape[1] // own_rows
    for place in range(out.shape[0]):
        if place < late:
            block = far[:, place * own_rows : (place + 1) * own_rows, :].astype(f32)
        else:
            block = near[:, (place - late) * own_rows : (place - late + 1) * own_rows, :].astype(f32)
        out[info[4 + place]] = jnp.sum(block, axis=0).astype(bf16)


def outer_kernel(places, rank, share, split, last, info, lows, ids, *refs):
    refs = list(refs)
    outs = [refs.pop() for _ in range(2 if last else 1)][::-1]
    before = refs.pop() if last else None
    chunks = refs
    if split:
        chunks = [(chunks[0][...], chunks[1][...])] + [(ref[0], ref[1]) for ref in chunks[2:]]
    else:
        chunks = [(ref[0], ref[1]) for ref in chunks]
    rows = chunks[0][0].shape[0]
    slot = lax.broadcasted_iota(jnp.int32, (share * rank, rows), 0) // rank
    half = share // 2
    tenant = share * info[3] + jnp.where(slot < half, 2 * slot + info[2], 2 * (slot - half) + 1 - info[2])
    for member in range(2):
        total = before[member] if last else 0.0
        for place, chunk in zip(places, chunks):
            values = lows[info[4 + place], member * rank : (member + 1) * rank, :].astype(f32)
            values = jnp.concatenate([values] * share, axis=0)
            chosen = jnp.where(tenant == ids[place : place + 1, :], values, 0.0).astype(bf16)
            total = total + dot(chosen, chunk[member])
        if last:
            outs[0][member] = total[: half * rank]
            outs[1][member] = total[half * rank :].astype(bf16)
        else:
            outs[0][member] = total


def on_device(tokens, tenant_ids, gate_weight, up_weight, adapter_in, adapter_out, grad_hidden):
    groups = lax.axis_size(GROUP)
    chips = lax.axis_size("y") * lax.axis_size("x")
    own_rows, _ = tokens.shape
    depth, columns = gate_weight.shape
    rank = adapter_out.shape[2]
    rows = chips * own_rows
    chip_columns = 2 * columns
    z = lax.axis_index(GROUP)
    c = lax.axis_index(CORE)
    u = lax.axis_index("y") * lax.axis_size("x") + lax.axis_index("x")
    first_core = c == 0
    order = jnp.array(ORDER, jnp.int32)
    group_at = (z + order) % groups
    swap = [(0, 1), (1, 0)]
    up_ring = [(i, (i + 1) % groups) for i in range(groups)]
    down_ring = [(i, (i - 1) % groups) for i in range(groups)]

    def other_core(value):
        return lax.ppermute(value, CORE, swap)

    def ring(value, pairs):
        return lax.ppermute(value, GROUP, pairs)

    def both(own, other):
        return jnp.where(first_core, own, other), jnp.where(first_core, other, own)

    ids = jnp.broadcast_to(tenant_ids.reshape(own_rows, 1, 1).astype(bf16), (own_rows, groups, 128))
    wide = jnp.concatenate([tokens.reshape(own_rows, groups, depth), ids], axis=2)
    sliced = lax.all_to_all(
        wide.reshape(own_rows, groups * (depth + 128)), GROUP, split_axis=1, concat_axis=0, tiled=True
    )
    sliced = pick(sliced.reshape(groups, own_rows, depth + 128), group_at)
    sliced = sliced.reshape(groups * own_rows, depth + 128)
    count = groups * own_rows
    id_columns = sliced[:, depth:]
    lane = lax.broadcasted_iota(jnp.int32, (count, 128), 1)
    row = lax.broadcasted_iota(jnp.int32, (count, 128), 0)
    id_lanes = jnp.sum(jnp.where(lane == row, id_columns.astype(f32), 0.0), axis=0, keepdims=True)
    id_block = jnp.broadcast_to(id_lanes.astype(bf16), (8, 128))
    tiles = sliced[:, :depth].reshape(groups, own_rows, depth // 128, 128).transpose(0, 2, 1, 3)
    tiles = tiles.reshape(count * (depth // 128), 128)
    gathered = spread(jnp.concatenate([tiles, id_block], axis=0), CHIPS, chips)
    row_ids = gathered[:, count * (depth // 128), :count].astype(f32).astype(jnp.int32)
    row_ids = row_ids.reshape(chips, groups, own_rows).transpose(1, 0, 2).reshape(groups, rows)

    info = jnp.concatenate([jnp.stack([2 * u + c, 2 * u + 1 - c, c, z]), group_at]).astype(jnp.int32)
    by_core = grad_hidden.reshape(chips, 2, own_rows, columns)
    give = lax.dynamic_index_in_dim(by_core, 1 - c, 1, keepdims=False)
    weight, upstream = call(
        join_kernel,
        info,
        [gate_weight, up_weight, other_core(gate_weight), other_core(up_weight), by_core, other_core(give)],
        [((2, depth, chip_columns), bf16), ((rows, chip_columns), bf16)],
    )

    inner = lax.dynamic_slice_in_dim(adapter_in[0], z * depth, depth, axis=1)
    inner = jnp.concatenate([inner, other_core(inner)], axis=0)
    outer = adapter_out.reshape(2 * rank, chips, chip_columns).transpose(1, 0, 2)
    outer = lax.all_to_all(outer, CHIPS, split_axis=0, concat_axis=0, tiled=True)
    outer = outer.reshape(chips, 2, rank, chip_columns)
    other_outer = other_core(outer)

    shape = (rows, chip_columns)
    going_up, going_down = call(
        functools.partial(first_kernel, own_rows), info, [gathered, weight], [(shape, bf16)] * 2
    )
    going_up = ring(going_up, up_ring)[None]
    going_down = ring(going_down, down_ring)[None]
    going_up = jnp.pad(going_up, ((0, 1), (0, 0), (0, 0)))
    going_down = jnp.pad(going_down, ((1, 0), (0, 0), (0, 0)))
    *pairs, product = call(
        functools.partial(rest_kernel, own_rows),
        info,
        [gathered, weight],
        [((count, 2) + shape, bf16) for count in (2, 2, 2, 1)],
    )
    for step, pair in enumerate(pairs, 2):
        going_up = (pair[0].astype(f32) + going_up.astype(f32)).astype(bf16)
        going_down = (pair[1].astype(f32) + going_down.astype(f32)).astype(bf16)
        going_up = ring(going_up, up_ring)
        going_down = ring(going_down, down_ring)

    (low_parts,) = call(
        functools.partial(low_kernel, own_rows), info, [gathered, inner, row_ids], [((groups, 2 * rank, rows), f32)]
    )
    low_here = lax.all_to_all(low_parts, GROUP, split_axis=0, concat_axis=0, tiled=True)
    low_here = jnp.sum(low_here, axis=0).astype(bf16)
    low = spread(low_here, CHIPS, chips)
    low = jnp.sum(low.astype(f32), axis=0).astype(bf16)

    slots = 2 * chips * rank
    hidden_rows, grads, grad_low = call(
        functools.partial(middle_kernel, rank),
        info,
        [product, going_up, going_down, outer, other_outer, low, row_ids, upstream],
        [(shape, bf16), ((2,) + shape, bf16), ((2 * rank, rows), bf16)],
        (pltpu.VMEM((2, rows, slots), bf16), pltpu.VMEM((2, slots, rows), f32)),
    )

    grads_at = {0: [grads]}
    below = ring(grads, up_ring)
    above = ring(grads, down_ring)
    grads_at[7], grads_at[1] = [below], [above]
    for step in (2, 3):
        below = ring(below, up_ring)
        above = ring(above, down_ring)
        grads_at[groups - step], grads_at[step] = [below], [above]
    grads_at[4] = [ring(below[0], up_ring), ring(above[1], down_ring)]

    halves = hidden_rows.reshape(chips, own_rows, 2, columns)
    keep = lax.dynamic_index_in_dim(halves, c, 2, keepdims=False)
    give = lax.dynamic_index_in_dim(halves, 1 - c, 2, keepdims=False)
    hidden = jnp.stack(both(keep, other_core(give)), axis=1).reshape(chips * 2 * own_rows, columns)

    grad_low = spread(grad_low, CHIPS, chips)
    grad_low = jnp.sum(grad_low.astype(f32), axis=0).astype(bf16)
    lows = jnp.concatenate([low, grad_low], axis=0)
    lows = spread(lows, GROUP, groups)

    def to_owners(first, last):
        count = last - first
        chunks = [array for d in ORDER[first:last] for array in grads_at[d]]
        (part,) = call(
            functools.partial(back_kernel, first, count, first == 0),
            info,
            [weight, inner, lows, row_ids] + chunks,
            [((chips, count * own_rows, depth), bf16)],
            (pltpu.VMEM((count * rows, inner.shape[0]), bf16),),
        )
        return lax.all_to_all(part, CHIPS, split_axis=0, concat_axis=0, tiled=True)

    near = to_owners(LATE, groups)
    far = to_owners(0, LATE)
    (summed,) = call(place_kernel, info, [near, far], [((groups, own_rows, depth), bf16)])
    grad_tokens = lax.all_to_all(
        summed.reshape(groups * own_rows, depth), GROUP, split_axis=0, concat_axis=1, tiled=True
    )

    (inner_grads,) = call(
        functools.partial(inner_kernel, own_rows), info, [gathered, lows, row_ids], [((4 * rank, depth), f32)]
    )
    grad_in = inner_grads[: 2 * rank] + other_core(inner_grads[2 * rank :])

    share = 2 * chips // groups

    def outer_grads(places, before):
        chunks = [array for place in places for array in grads_at[ORDER[place]]]
        arrays = [lows, row_ids] + chunks + ([] if before is None else [before])
        full = (2, share * rank, chip_columns)
        part = (2, share // 2 * rank, chip_columns)
        outs = [(full, f32)] if before is None else [(part, f32), (part, bf16)]
        return call(
            functools.partial(outer_kernel, places, rank, share, 0 in places, before is not None), info, arrays, outs
        )

    (outs,) = outer_grads(tuple(range(LATE, groups)), None)
    keep, give = outer_grads(tuple(range(LATE)), outs)
    outs = (keep + other_core(give).astype(f32)).astype(bf16)
    outs = outs.reshape(2, share // 2, rank, chip_columns)
    lower = u % 2
    same = lax.dynamic_index_in_dim(outs, lower, 1, keepdims=False)
    cross = lax.dynamic_index_in_dim(outs, 1 - lower, 1, keepdims=False)
    straight, crossed = [], []
    for from_z in range(groups):
        for from_u in range(chips):
            source, low_bit = from_z * chips + from_u, from_u % 2
            target = (from_u // 2) * chips + 2 * from_z
            straight.append((source, target + low_bit))
            crossed.append((source, target + 1 - low_bit))
    same = lax.ppermute(same, (GROUP,) + CHIPS, straight)
    cross = lax.ppermute(cross, (GROUP,) + CHIPS, crossed)
    left = jnp.where(lower == 0, same, cross)
    right = jnp.where(lower == 0, cross, same)
    grad_out = adapter_scale * jnp.concatenate([left, right], axis=2).astype(f32)
    return hidden, grad_tokens, grad_in[None], grad_out[None]


def solution(mesh):
    groups, tenants = mesh.shape["dp"], mesh.shape["tenant"]
    split = Mesh(mesh.devices.reshape(groups, tenants // 8, 4, 2), ("z", "y", "x", "c"))
    tenant = ("y", "x", "c")
    in_specs = (
        P(("z",) + tenant, None),
        P("z", tenant),
        P("z", tenant),
        P("z", tenant),
        P(tenant, None, None),
        P(tenant, None, None, None),
        P("z", tenant),
    )
    out_specs = (
        P("z", tenant),
        P(("z",) + tenant, None),
        P(tenant, None, "z"),
        P(tenant, None, None, "z"),
    )
    return jax.shard_map(on_device, mesh=split, in_specs=in_specs, out_specs=out_specs, check_vma=False)
```
